512 devices in a mesh: sta: 8 (over z_hi, x), tm: 64 (over y, z_lo, core).
Axes of the slice: x: 4, y: 8, z: 8 (z_hi: 2, z_lo: 4; z = z_hi * 4 + z_lo), core: 2. Of those that a mesh axis runs over, the one named last changes fastest.
Arguments:
- record: bfloat16 [96, 49152], P('sta', 'tm')
- templates: bfloat16 [64, 96, 512], P('tm', 'sta'), may hold values from -6 to 6
- shifts: int32 [96], P('sta'), may hold values from 0 to 255, as said below
- live_mask: int32 [96], P('sta'), may hold values 0 or 1
- plan: int32 [64], replicated, may hold values from 0 to 63, each once
Outputs:
- stacks: float32 [64, 49152], P('sta', 'tm')
The draws below stay inside these ranges and needn't reach their ends.
Inputs may be any that keep to these rules, and one draw needn't show every extreme that they name: `shifts`: some channel has the shift 256 - 1. `plan`: each bank slot appears once.
All inputs are finite; a program needn't handle non-finite values. No bound on the sum of `live_mask` on one device may be relied on, other than what follows from the above.
Results may differ from the reference program's by a relative error of at most 0.0003.
Values may be sent and summed in bfloat16 or wider, within the bound.
A program may use at most 64 MiB of HBM per device.

```python
import math
import jax
import jax.numpy as jnp
from jax import lax

TEMPLATES = 64
CHANNELS = 96
TAPS = 512
MAX_SHIFT = 256
SAMPLES = 49152


def draw_record(key, part):
    key_base, key_chan, key_env = jax.random.split(key, 3)
    noise_base = jax.random.normal(key_base, (CHANNELS, SAMPLES), jnp.float32)
    chan_scale = jnp.exp(jax.random.uniform(key_chan, (CHANNELS, 1), jnp.float32) * math.log(10.0))
    envelope = jnp.exp(jax.random.uniform(key_env, (CHANNELS, SAMPLES // 64), jnp.float32, -1.0, 1.0) * math.log(3.0))
    envelope = jnp.repeat(envelope, 64, axis=1)
    return (noise_base * chan_scale * envelope).astype(jnp.bfloat16)


def draw_shifts(key, part):
    key_lags, key_pin = jax.random.split(key, 2)
    lag_draw = jax.random.randint(key_lags, (CHANNELS,), 0, MAX_SHIFT)
    pinned = jax.random.randint(key_pin, (), 0, CHANNELS)
    return lag_draw.at[pinned].set(MAX_SHIFT - 1).astype(jnp.int32)


def touch_ends(result, own_key, least, high):
    extent = result.shape
    place = [jax.random.randint(jax.random.fold_in(own_key, axis), (), 0, extent[axis]) for axis in range(len(extent))]
    result = result.at[tuple(place)].set(least)
    longest = extent.index(max(extent))
    place[longest] = (place[longest] + 1) % extent[longest]
    return result.at[tuple(place)].set(high)


def level_of(stream_key, extent, pieces, smallest, top_value):
    gain, own = 1.0, jax.random.fold_in(stream_key, 6)
    for axis_at, blocks in pieces:
        steps = jnp.exp(jax.random.uniform(jax.random.fold_in(own, axis_at), (blocks,), jnp.float32, smallest / len(pieces), top_value / len(pieces)))
        gain = gain * jnp.repeat(steps, extent[axis_at] // blocks).reshape([-1 if axis == axis_at else 1 for axis in range(len(extent))])
    return gain


def centred(own_key, extent, width, reach, pieces=(), held_as=jnp.bfloat16):
    values = jax.random.normal(own_key, extent, jnp.float32) * width
    if len(pieces) > 0:
        values = level_of(own_key, extent, pieces, -0.22, 0.18) * values
    return jnp.clip(values, min=-reach, max=reach).astype(held_as)


def setup_inputs(seed: int = 0) -> dict:
    keys = jax.random.split(jax.random.key(seed), 6)
    record = draw_record(jax.random.fold_in(keys[5], 71), 0)
    templates = centred(keys[1], (TEMPLATES, CHANNELS, TAPS), 1.0, 6.0, ((0, 64), (1, 8)))
    shifts = draw_shifts(jax.random.fold_in(keys[5], 71), 0)
    live_mask = touch_ends((jax.random.randint(keys[3], (CHANNELS,), 0, 4) < 3).astype(jnp.int32), jax.random.fold_in(keys[3], 1), 0, 1)
    plan = jax.random.permutation(keys[4], TEMPLATES).astype(jnp.int32)
    return dict(record=record, templates=templates, shifts=shifts, live_mask=live_mask, plan=plan)


def reference(record, templates, shifts, live_mask, plan):
    signal = record.astype(jnp.float32)
    padded = jnp.pad(signal, ((0, 0), (0, MAX_SHIFT + TAPS)))
    total_len = SAMPLES + TAPS
    overall = math.sqrt(TAPS / CHANNELS)

    def add_channel(chan_idx, running):
        signal_row = lax.dynamic_index_in_dim(padded, chan_idx, 0, keepdims=False)
        window = lax.dynamic_slice_in_dim(signal_row, shifts[chan_idx].astype(jnp.int32), total_len)
        copies = jnp.tile(window, TAPS + 1)
        hankel = copies[:TAPS * (total_len + 1)].reshape(TAPS, total_len + 1)[:, :SAMPLES]
        panel_rows = lax.dynamic_index_in_dim(templates, chan_idx, 1, keepdims=False).astype(jnp.float32)
        products = jnp.dot(panel_rows, hankel, precision=lax.Precision.HIGHEST)
        energy = lax.optimization_barrier(jnp.sum(hankel * hankel, axis=0))
        norm_vals = jnp.sqrt(lax.optimization_barrier(jnp.sum(panel_rows * panel_rows, axis=1)) + 1e-06)
        weighting = live_mask[chan_idx].astype(jnp.float32) * overall / norm_vals
        return running + products * weighting[:, None] * lax.rsqrt(energy + 1e-06)[None, :]
    running = lax.fori_loop(0, CHANNELS, add_channel, jnp.zeros((TEMPLATES, SAMPLES), jnp.float32))
    return jnp.take(running, plan, axis=0)
```

```python
import functools
import math

import jax
import jax.numpy as jnp
from jax import lax
from jax.experimental import pallas as pl
from jax.experimental.pallas import tpu as pltpu
from jax.sharding import PartitionSpec as P

CHANNELS = 96
ZRUN = 4
ZHALVES = 2
MESH = pl.DeviceIdType.MESH


def shifted_left(value, by):
    width = value.shape[1]
    if by % width == 0:
        return value
    return pltpu.roll(value, width - by, 1)


def stack_kernel(
    sizes,
    record,
    templates,
    shifts,
    live,
    plan,
    out,
    rec_buf,
    halo,
    bank,
    wave,
    hankel,
    gain,
    aligned,
    total,
    row_recv,
    far_send,
    far_recv,
    shift_s,
    live_s,
    plan_s,
    load_sem,
    halo_sem,
    send_sem,
    recv_sem,
    pair_send,
    pair_recv,
    row_ssem,
    row_rsem,
    far_sem,
):
    rows_y, cols_x, chans, span, taps = sizes
    count = rows_y * ZRUN * 2
    ext = 2 * span
    reach = span + taps
    sta = lax.axis_index("sta")
    me = lax.axis_index("tm")
    core = me % 2
    at_z = (me // 2) % ZRUN
    at_y = me // (2 * ZRUN)
    at_x = sta % cols_x
    half = sta // cols_x

    def slot(y, z, c):
        return (y * ZRUN + z) * 2 + c

    after, before = (me + 1) % count, (me + count - 1) % count
    partner = slot(at_y, at_z, 1 - core)
    y_peers = [slot((at_y + d) % rows_y, at_z, core) for d in range(1, rows_y)]
    z_peers = [slot(at_y, (at_z + d) % ZRUN, core) for d in range(1, ZRUN)]
    x_peers = [half * cols_x + (at_x + d) % cols_x for d in range(1, cols_x)]
    far_peer = (1 - half) * cols_x + at_x
    outer = jnp.where(core == 0, before, after)

    loads = [
        pltpu.make_async_copy(record, rec_buf, load_sem.at[0]),
        pltpu.make_async_copy(templates.at[0], bank.at[me], load_sem.at[1]),
        pltpu.make_async_copy(shifts, shift_s, load_sem.at[2]),
        pltpu.make_async_copy(live, live_s, load_sem.at[3]),
        pltpu.make_async_copy(plan, plan_s, load_sem.at[4]),
    ]
    for load in loads:
        load.start()

    barrier = pltpu.get_barrier_semaphore()
    met = [{"tm": p} for p in y_peers + z_peers + [partner, outer]]
    met += [{"sta": p} for p in x_peers + [far_peer]]
    for peer in met:
        pl.semaphore_signal(barrier, inc=1, device_id=peer, device_id_type=MESH)
    pl.semaphore_wait(barrier, len(met))

    def piece_copy(src, owner, target, sem_at):
        return pltpu.make_async_remote_copy(
            src_ref=src,
            dst_ref=bank.at[owner],
            send_sem=send_sem.at[sem_at],
            recv_sem=recv_sem.at[owner],
            device_id={"tm": target},
            device_id_type=MESH,
        )

    def pair_copy(src, owner, sem_at):
        return pltpu.make_async_remote_copy(
            src_ref=src,
            dst_ref=bank.at[owner],
            send_sem=pair_send.at[sem_at],
            recv_sem=pair_recv.at[owner],
            device_id={"tm": partner},
            device_id_type=MESH,
        )

    own = templates.at[0]
    z_steps = [1, 3, 2]
    y_steps = [4, 3, 5, 2, 6, 1, 7] if rows_y == 8 else list(range(1, rows_y))
    firsts = []
    for at, d in enumerate(z_steps):
        firsts.append(piece_copy(own, me, slot(at_y, (at_z + d) % ZRUN, core), at))
    for at, d in enumerate(y_steps):
        firsts.append(piece_copy(own, me, slot((at_y + d) % rows_y, at_z, core), len(z_steps) + at))
    for copy in firsts:
        copy.start()
    halo_copy = pltpu.make_async_remote_copy(
        src_ref=record,
        dst_ref=halo,
        send_sem=halo_sem.at[0],
        recv_sem=halo_sem.at[1],
        device_id={"tm": before},
        device_id_type=MESH,
    )
    halo_copy.start()
    own_pair = pair_copy(own, me, 0)
    own_pair.start()

    n_first = len(z_steps) + len(y_steps)

    @pl.when(core == 0)
    def _():
        at = n_first
        for back in [3, 1, 2]:
            owner = slot(at_y, (at_z + back) % ZRUN, core)
            piece_copy(bank.at[owner], owner, me, 0).wait_recv()
            for d in y_steps:
                target = slot((at_y + d) % rows_y, at_z, core)
                piece_copy(bank.at[owner], owner, target, at).start()
                at += 1

    @pl.when(core == 1)
    def _():
        at = n_first
        for back in [7, 1, 6, 2, 5, 3, 4]:
            owner = slot((at_y + back) % rows_y, at_z, core)
            piece_copy(bank.at[owner], owner, me, 0).wait_recv()
            for d in z_steps:
                target = slot(at_y, (at_z + d) % ZRUN, core)
                piece_copy(bank.at[owner], owner, target, at).start()
                at += 1

    halo_copy.wait_recv()
    for load in loads:
        load.wait()

    row16 = lax.broadcasted_iota(jnp.int32, (16, ext), 0)
    lag = jnp.zeros((16, ext), jnp.int32)
    for c in range(chans):
        lag = jnp.where(row16 == c, shift_s[c], lag)
    tail = jnp.where(me == count - 1, 0.0, halo[...].astype(jnp.float32))
    signal = jnp.concatenate([rec_buf[...].astype(jnp.float32), tail], axis=1)
    signal = jnp.concatenate([signal, jnp.zeros((16 - chans, ext), jnp.float32)], axis=0)
    for bit in range(8):
        signal = jnp.where(
            (lag & (1 << bit)) != 0, shifted_left(signal, 1 << bit), signal
        )
    signal = signal[:, :reach]
    aligned[...] = signal
    energy = signal * signal
    step = 1
    while step < taps:
        energy = energy + shifted_left(energy, step)
        step *= 2
    gain[...] = lax.rsqrt(energy[:, :span] + 1e-06)

    row8 = lax.broadcasted_iota(jnp.int32, (8, reach), 0)
    wide = span + taps // 2

    def build(c, carry):
        lanes = jnp.broadcast_to(aligned[pl.ds(c, 1), :], (8, reach))
        for bit in range(3):
            lanes = jnp.where((row8 & (1 << bit)) != 0, shifted_left(lanes, 1 << bit), lanes)
        for q in range(8):
            pair = jnp.concatenate(
                [shifted_left(lanes, 16 * q), shifted_left(lanes, 16 * q + 8)], axis=0
            ).astype(jnp.bfloat16)
            hankel[c, 16 * q : 16 * q + 16, :] = pair[:, :wide]
            hankel[c, 128 + 16 * q : 144 + 16 * q, :] = pair[:, 128 : 128 + wide]
        return carry

    lax.fori_loop(0, chans, build, 0)

    at = 1
    mine = []
    for dz in [0, 1, 3, 2]:
        for dy in [0, 7, 1, 6, 2, 5, 3, 4] if rows_y == 8 else range(rows_y):
            if dz or dy:
                mine.append(((at_z + dz) % ZRUN, (at_y + dy) % rows_y, dz == 0, dy == 0))
    for z, y, same_z, same_y in mine:
        owner = slot(y, z, core)
        relayed = jnp.where(core == 0, same_y, same_z)

        @pl.when(jnp.logical_not(relayed))
        def _():
            piece_copy(bank.at[owner], owner, me, 0).wait_recv()

        pair_copy(bank.at[owner], owner, at).start()
        at += 1

    for y in range(rows_y):
        for z in range(ZRUN):
            owner = slot(y, z, 1 - core)
            pair_copy(bank.at[owner], owner, 0).wait_recv()

    def widen(p, carry):
        piece = bank[plan_s[p]].astype(jnp.float32)
        for part in range(taps // 128):
            wave[part, pl.ds(pl.multiple_of(p * 16, 16), chans), :] = piece[
                :, part * 128 : part * 128 + 128
            ]
        return carry

    lax.fori_loop(0, count, widen, 0)

    overall = math.sqrt(taps / CHANNELS)
    total[...] = jnp.zeros_like(total)

    def channel(c, carry):
        panel = jnp.concatenate(
            [wave[part, pl.ds(c, count, stride=16), :] for part in range(taps // 128)], axis=1
        )
        norm = jnp.sum(panel * panel, axis=1, keepdims=True)
        weight = (live_s[c].astype(jnp.float32) * overall) * lax.rsqrt(norm + 1e-06)
        panel = panel.astype(jnp.bfloat16)
        corr = jnp.dot(
            panel[:, : taps // 2], hankel[c, :, :span], preferred_element_type=jnp.float32
        ) + jnp.dot(
            panel[:, taps // 2 :],
            hankel[c, :, taps // 2 : taps // 2 + span],
            preferred_element_type=jnp.float32,
        )
        total[...] += corr * weight * gain[pl.ds(c, 1), :]
        return carry

    lax.fori_loop(0, chans, channel, 0)

    per = count // (cols_x * ZHALVES)

    def block(h, x):
        return total.at[pl.ds(pl.multiple_of((h * cols_x + x) * per, per), per), :]

    def row_copy(far, d):
        h = 1 - half if far else half
        kind = 0 if far else 1
        return pltpu.make_async_remote_copy(
            src_ref=block(h, (at_x + d) % cols_x),
            dst_ref=row_recv.at[kind, d - 1],
            send_sem=row_ssem.at[kind, d - 1],
            recv_sem=row_rsem.at[kind, d - 1],
            device_id={"sta": half * cols_x + (at_x + d) % cols_x},
            device_id_type=MESH,
        )

    x_steps = [2, 1, 3] if cols_x == 4 else list(range(1, cols_x))
    row_copies = [row_copy(far, d) for far in (True, False) for d in x_steps]
    for copy in row_copies:
        copy.start()
    for copy in row_copies[: len(x_steps)]:
        copy.wait_recv()
    far_send[...] = block(1 - half, at_x)[...] + sum(
        row_recv[0, d - 1] for d in range(1, cols_x)
    )
    far_copy = pltpu.make_async_remote_copy(
        src_ref=far_send,
        dst_ref=far_recv,
        send_sem=far_sem.at[0],
        recv_sem=far_sem.at[1],
        device_id={"sta": far_peer},
        device_id_type=MESH,
    )
    far_copy.start()
    for copy in row_copies[len(x_steps) :]:
        copy.wait_recv()
    near = block(half, at_x)[...] + sum(row_recv[1, d - 1] for d in range(1, cols_x))
    far_copy.wait_recv()
    out[...] = near + far_recv[...]

    for copy in row_copies + [far_copy, halo_copy]:
        copy.wait_send()
    for at in range(n_first + 21 if rows_y == 8 else n_first):
        piece_copy(own, me, me, at).wait_send()
    for at in range(rows_y * ZRUN):
        pair_copy(own, me, at).wait_send()


def per_device(rows_y, cols_x, record, templates, shifts, live, plan):
    chans, span = record.shape
    taps = templates.shape[2]
    count = plan.shape[0]
    per = count // (cols_x * ZHALVES)
    any_spec = pl.BlockSpec(memory_space=pl.ANY)
    dma = pltpu.SemaphoreType.DMA
    pieces = rows_y * ZRUN
    return pl.pallas_call(
        functools.partial(stack_kernel, (rows_y, cols_x, chans, span, taps)),
        out_shape=jax.ShapeDtypeStruct((per, span), jnp.float32),
        in_specs=[any_spec] * 5,
        out_specs=pl.BlockSpec(memory_space=pltpu.VMEM),
        scratch_shapes=[
            pltpu.VMEM((chans, span), jnp.bfloat16),
            pltpu.VMEM((chans, span), jnp.bfloat16),
            pltpu.VMEM((count, chans, taps), jnp.bfloat16),
            pltpu.VMEM((taps // 128, count * 16, 128), jnp.float32),
            pltpu.VMEM((chans, taps // 2, span + taps // 2), jnp.bfloat16),
            pltpu.VMEM((16, span), jnp.float32),
            pltpu.VMEM((16, span + taps), jnp.float32),
            pltpu.VMEM((count, span), jnp.float32),
            pltpu.VMEM((2, cols_x - 1, per, span), jnp.float32),
            pltpu.VMEM((per, span), jnp.float32),
            pltpu.VMEM((per, span), jnp.float32),
            pltpu.SMEM(shifts.shape, jnp.int32),
            pltpu.SMEM(live.shape, jnp.int32),
            pltpu.SMEM(plan.shape, jnp.int32),
            dma((5,)),
            dma((2,)),
            dma((pieces - 1,)),
            dma((count,)),
            dma((pieces,)),
            dma((count,)),
            dma((2, cols_x - 1)),
            dma((2, cols_x - 1)),
            dma((2,)),
        ],
        compiler_params=pltpu.CompilerParams(
            collective_id=0, has_side_effects=True, vmem_limit_bytes=40 * 2**20
        ),
    )(record, templates, shifts, live, plan)


def solution(mesh):
    cols_x = mesh.shape["sta"] // ZHALVES
    rows_y = mesh.shape["tm"] // (2 * ZRUN)
    placed = (P("sta", "tm"), P("tm", "sta", None), P("sta"), P("sta"), P())
    return jax.shard_map(
        functools.partial(per_device, rows_y, cols_x),
        mesh=mesh,
        in_specs=placed,
        out_specs=P("sta", "tm"),
        check_vma=False,
    )
```

```python
import functools
import math

import jax
import jax.numpy as jnp
from jax import lax
from jax.experimental import pallas as pl
from jax.experimental.pallas import tpu as pltpu
from jax.sharding import PartitionSpec as P

CHANNELS = 96
ZRUN = 4
ZHALVES = 2
MESH = pl.DeviceIdType.MESH


def shifted_left(value, by):
    width = value.shape[1]
    if by % width == 0:
        return value
    return pltpu.roll(value, width - by, 1)


def stack_kernel(
    sizes,
    record,
    templates,
    shifts,
    live,
    plan,
    out,
    rec_buf,
    halo,
    bank,
    wave,
    hankel,
    gain,
    aligned,
    total,
    row_recv,
    shift_s,
    live_s,
    plan_s,
    load_sem,
    halo_sem,
    send_sem,
    recv_sem,
    pair_sem,
    row_ssem,
    row_rsem,
):
    rows_y, cols_x, chans, span, taps = sizes
    count = rows_y * ZRUN * 2
    ext = 2 * span
    reach = span + taps
    sta = lax.axis_index("sta")
    me = lax.axis_index("tm")
    core = me % 2
    at_z = (me // 2) % ZRUN
    at_y = me // (2 * ZRUN)
    at_x = sta % cols_x
    half = sta // cols_x

    def slot(y, z, c):
        return (y * ZRUN + z) * 2 + c

    def place(y, z, c):
        return (c * rows_y + y) * ZRUN + z

    after, before = (me + 1) % count, (me + count - 1) % count
    partner = slot(at_y, at_z, 1 - core)
    y_peers = [slot((at_y + d) % rows_y, at_z, core) for d in range(1, rows_y)]
    z_peers = [slot(at_y, (at_z + d) % ZRUN, core) for d in range(1, ZRUN)]
    x_peers = [half * cols_x + (at_x + d) % cols_x for d in range(1, cols_x)]
    far_peers = [(1 - half) * cols_x + (at_x + d) % cols_x for d in range(cols_x)]
    outer = jnp.where(core == 0, before, after)

    barrier = pltpu.get_barrier_semaphore()
    met = [{"sta": p} for p in x_peers + far_peers]
    met += [{"tm": p} for p in y_peers + z_peers + [partner, outer]]
    for peer in met:
        pl.semaphore_signal(barrier, inc=1, device_id=peer, device_id_type=MESH)

    mine = place(at_y, at_z, core)
    loads = [
        pltpu.make_async_copy(record, rec_buf, load_sem.at[0]),
        pltpu.make_async_copy(templates.at[0], bank.at[mine], load_sem.at[1]),
        pltpu.make_async_copy(shifts, shift_s, load_sem.at[2]),
        pltpu.make_async_copy(live, live_s, load_sem.at[3]),
        pltpu.make_async_copy(plan, plan_s, load_sem.at[4]),
    ]
    for load in loads:
        load.start()

    pl.semaphore_wait(barrier, len(met))

    def piece_copy(src, index, sem, target):
        return pltpu.make_async_remote_copy(
            src_ref=src,
            dst_ref=bank.at[index],
            send_sem=send_sem.at[0],
            recv_sem=recv_sem.at[sem],
            device_id={"tm": target},
            device_id_type=MESH,
        )

    def group_wait(y, first, size, sem):
        group = bank.at[pl.ds(first, size)]
        pltpu.make_async_remote_copy(
            src_ref=group,
            dst_ref=group,
            send_sem=send_sem.at[0],
            recv_sem=recv_sem.at[sem],
            device_id={"tm": me},
            device_id_type=MESH,
        ).wait_recv()

    own = templates.at[0]
    z_steps = list(range(1, ZRUN))
    y_steps = sorted(range(1, rows_y), key=lambda d: -min(d, rows_y - d))
    z_sem = jnp.where(core == 0, at_z, rows_y + at_y)
    y_sem = jnp.where(core == 0, rows_y + at_y, at_y)

    def own_to_z():
        for d in z_steps:
            piece_copy(own, mine, z_sem, slot(at_y, (at_z + d) % ZRUN, core)).start()

    def own_to_y():
        for d in y_steps:
            piece_copy(own, mine, y_sem, slot((at_y + d) % rows_y, at_z, core)).start()

    @pl.when(core == 0)
    def _():
        own_to_z()
        own_to_y()

    @pl.when(core == 1)
    def _():
        own_to_y()
        own_to_z()

    halo_copy = pltpu.make_async_remote_copy(
        src_ref=record,
        dst_ref=halo,
        send_sem=halo_sem.at[0],
        recv_sem=halo_sem.at[1],
        device_id={"tm": before},
        device_id_type=MESH,
    )
    halo_copy.start()

    @pl.when(core == 0)
    def _():
        for back in [3, 1, 2]:
            z = (at_z + back) % ZRUN
            index = place(at_y, z, core)
            piece_copy(bank.at[index], index, z, me).wait_recv()
            for d in y_steps:
                target = slot((at_y + d) % rows_y, at_z, core)
                piece_copy(bank.at[index], index, rows_y + at_y, target).start()

    @pl.when(core == 1)
    def _():
        for back in y_steps[::-1]:
            y = (at_y + back) % rows_y
            index = place(y, at_z, core)
            piece_copy(bank.at[index], index, y, me).wait_recv()
            for d in z_steps:
                target = slot(at_y, (at_z + d) % ZRUN, core)
                piece_copy(bank.at[index], index, rows_y + y, target).start()

    halo_copy.wait_recv()
    for load in loads:
        load.wait()

    row16 = lax.broadcasted_iota(jnp.int32, (16, ext), 0)
    lag = jnp.zeros((16, ext), jnp.int32)
    for c in range(chans):
        lag = jnp.where(row16 == c, shift_s[c], lag)
    tail = jnp.where(me == count - 1, 0.0, halo[...].astype(jnp.float32))
    signal = jnp.concatenate([rec_buf[...].astype(jnp.float32), tail], axis=1)
    signal = jnp.concatenate([signal, jnp.zeros((16 - chans, ext), jnp.float32)], axis=0)
    for bit in range(8):
        signal = jnp.where(
            (lag & (1 << bit)) != 0, shifted_left(signal, 1 << bit), signal
        )
    signal = signal[:, :reach]
    aligned[...] = signal
    energy = signal * signal
    step = 1
    while step < taps:
        energy = energy + shifted_left(energy, step)
        step *= 2
    gain[...] = lax.rsqrt(energy[:, :span] + 1e-06)

    row8 = lax.broadcasted_iota(jnp.int32, (8, reach), 0)
    wide = span + taps // 2

    def build(c, carry):
        lanes = jnp.broadcast_to(aligned[pl.ds(c, 1), :], (8, reach))
        for bit in range(3):
            lanes = jnp.where((row8 & (1 << bit)) != 0, shifted_left(lanes, 1 << bit), lanes)
        for q in range(8):
            pair = jnp.concatenate(
                [shifted_left(lanes, 16 * q), shifted_left(lanes, 16 * q + 8)], axis=0
            ).astype(jnp.bfloat16)
            hankel[c, 16 * q : 16 * q + 16, :] = pair[:, :wide]
            hankel[c, 128 + 16 * q : 144 + 16 * q, :] = pair[:, 128 : 128 + wide]
        return carry

    lax.fori_loop(0, chans, build, 0)

    def hand_over(y):
        group = bank.at[pl.ds(place(y, 0, core), ZRUN)]
        pltpu.make_async_remote_copy(
            src_ref=group,
            dst_ref=group,
            send_sem=pair_sem.at[0],
            recv_sem=pair_sem.at[1],
            device_id={"tm": partner},
            device_id_type=MESH,
        ).start()

    for d in [0] + y_steps[::-1]:
        y = (at_y + d) % rows_y
        base = place(y, 0, core)
        if d:

            @pl.when(core == 0)
            def _():
                group_wait(y, base, ZRUN, rows_y + y)

        @pl.when(core == 1)
        def _():
            group_wait(y, base, ZRUN - 1, rows_y + y)

        hand_over(y)

    pieces = rows_y * ZRUN
    theirs = bank.at[pl.ds((1 - core) * pieces, pieces)]
    handed = pltpu.make_async_remote_copy(
        src_ref=theirs,
        dst_ref=theirs,
        send_sem=pair_sem.at[0],
        recv_sem=pair_sem.at[1],
        device_id={"tm": me},
        device_id_type=MESH,
    )
    handed.wait_recv()

    def widen(p, carry):
        piece = bank[(plan_s[p] % 2) * pieces + plan_s[p] // 2].astype(jnp.float32)
        for part in range(taps // 128):
            wave[part, pl.ds(pl.multiple_of(p * 16, 16), chans), :] = piece[
                :, part * 128 : part * 128 + 128
            ]
        return carry

    overall = math.sqrt(taps / CHANNELS)
    some = count // ZHALVES

    def stack(first):
        lax.fori_loop(0, some, lambda i, carry: widen(first + i, carry), 0, unroll=4)
        running = jnp.zeros((some, span), jnp.float32)
        for c in range(chans):
            panel = jnp.concatenate(
                [wave[part, pl.ds(first * 16 + c, some, stride=16), :] for part in range(taps // 128)],
                axis=1,
            )
            norm = jnp.sum(panel * panel, axis=1, keepdims=True)
            weight = (live_s[c].astype(jnp.float32) * overall) * lax.rsqrt(norm + 1e-06)
            panel = panel.astype(jnp.bfloat16)
            half_taps = taps // 2
            both = jnp.concatenate([panel[:, :half_taps], panel[:, half_taps:]], axis=0)
            tiles = span // half_taps
            parts = []
            for t in range(tiles + 1):
                rows = both[:some] if t == 0 else both[some:] if t == tiles else both
                parts.append(
                    jnp.dot(
                        rows,
                        hankel[c, :, t * half_taps : (t + 1) * half_taps],
                        preferred_element_type=jnp.float32,
                    )
                )
            corr = jnp.concatenate(
                [parts[t][:some] + parts[t + 1][-some:] for t in range(tiles)], axis=1
            )
            running = running + corr * weight * gain[c : c + 1, :]
        total[pl.ds(pl.multiple_of(first, some), some), :] = running

    per = count // (cols_x * ZHALVES)

    def block(h, x):
        return total.at[pl.ds(pl.multiple_of((h * cols_x + x) * per, per), per), :]

    def row_copy(far, d):
        h = 1 - half if far else half
        kind = 0 if far else 1
        return pltpu.make_async_remote_copy(
            src_ref=block(h, (at_x + d) % cols_x),
            dst_ref=row_recv.at[kind, d],
            send_sem=row_ssem.at[kind, d],
            recv_sem=row_rsem.at[kind, d],
            device_id={"sta": h * cols_x + (at_x + d) % cols_x},
            device_id_type=MESH,
        )

    x_steps = [2, 1, 3, 0] if cols_x == 4 else list(range(cols_x))
    stack((1 - half) * some)
    far_copies = [row_copy(True, d) for d in x_steps]
    for copy in far_copies:
        copy.start()
    stack(half * some)
    near_copies = [row_copy(False, d) for d in x_steps if d]
    for copy in near_copies:
        copy.start()
    sent = bank.at[pl.ds(0, pieces - 1)]
    pltpu.make_async_remote_copy(
        src_ref=sent,
        dst_ref=sent,
        send_sem=send_sem.at[0],
        recv_sem=recv_sem.at[0],
        device_id={"tm": me},
        device_id_type=MESH,
    ).wait_send()
    handed.wait_send()
    halo_copy.wait_send()
    for copy in near_copies:
        copy.wait_recv()
    near = block(half, at_x)[...] + sum(row_recv[1, d] for d in range(1, cols_x))
    for copy in far_copies:
        copy.wait_recv()
    out[...] = near + sum(row_recv[0, d] for d in range(cols_x))
    for copy in far_copies + near_copies:
        copy.wait_send()


def per_device(rows_y, cols_x, record, templates, shifts, live, plan):
    chans, span = record.shape
    taps = templates.shape[2]
    count = plan.shape[0]
    per = count // (cols_x * ZHALVES)
    any_spec = pl.BlockSpec(memory_space=pl.ANY)
    dma = pltpu.SemaphoreType.DMA
    return pl.pallas_call(
        functools.partial(stack_kernel, (rows_y, cols_x, chans, span, taps)),
        out_shape=jax.ShapeDtypeStruct((per, span), jnp.float32),
        in_specs=[any_spec] * 5,
        out_specs=pl.BlockSpec(memory_space=pltpu.VMEM),
        scratch_shapes=[
            pltpu.VMEM((chans, span), jnp.bfloat16),
            pltpu.VMEM((chans, span), jnp.bfloat16),
            pltpu.VMEM((count, chans, taps), jnp.bfloat16),
            pltpu.VMEM((taps // 128, count * 16, 128), jnp.float32),
            pltpu.VMEM((chans, taps // 2, span + taps // 2), jnp.bfloat16),
            pltpu.VMEM((16, span), jnp.float32),
            pltpu.VMEM((16, span + taps), jnp.float32),
            pltpu.VMEM((count, span), jnp.float32),
            pltpu.VMEM((2, cols_x, per, span), jnp.float32),
            pltpu.SMEM(shifts.shape, jnp.int32),
            pltpu.SMEM(live.shape, jnp.int32),
            pltpu.SMEM(plan.shape, jnp.int32),
            dma((5,)),
            dma((2,)),
            dma((1,)),
            dma((2 * rows_y,)),
            dma((2,)),
            dma((2, cols_x)),
            dma((2, cols_x)),
        ],
        compiler_params=pltpu.CompilerParams(
            collective_id=0, has_side_effects=True, vmem_limit_bytes=67043328
        ),
    )(record, templates, shifts, live, plan)


def solution(mesh):
    cols_x = mesh.shape["sta"] // ZHALVES
    rows_y = mesh.shape["tm"] // (2 * ZRUN)
    placed = (P("sta", "tm"), P("tm", "sta", None), P("sta"), P("sta"), P())
    return jax.shard_map(
        functools.partial(per_device, rows_y, cols_x),
        mesh=mesh,
        in_specs=placed,
        out_specs=P("sta", "tm"),
        check_vma=False,
    )
```

```python
import functools
import math

import jax
import jax.numpy as jnp
from jax import lax
from jax.experimental import pallas as pl
from jax.experimental.pallas import tpu as pltpu
from jax.sharding import PartitionSpec as P

CHANNELS = 96
ZRUN = 4
ZHALVES = 2
Z_ORDER = (1, 3, 2)
MESH = pl.DeviceIdType.MESH


def shifted_left(value, by):
    width = value.shape[1]
    if by % width == 0:
        return value
    return pltpu.roll(value, width - by, 1)


def stack_kernel(
    sizes,
    record,
    templates,
    shifts,
    live,
    plan,
    out,
    rec_buf,
    halo,
    bank,
    wave,
    weights,
    hankel,
    gain,
    aligned,
    total,
    row_recv,
    shift_s,
    live_s,
    plan_s,
    load_sem,
    halo_sem,
    send_sem,
    recv_sem,
    pair_sem,
    row_ssem,
    row_rsem,
):
    rows_y, cols_x, chans, span, taps = sizes
    count = rows_y * ZRUN * 2
    ext = 2 * span
    reach = span + taps
    sta = lax.axis_index("sta")
    me = lax.axis_index("tm")
    core = me % 2
    at_z = (me // 2) % ZRUN
    at_y = me // (2 * ZRUN)
    at_x = sta % cols_x
    half = sta // cols_x

    def slot(y, z, c):
        return (y * ZRUN + z) * 2 + c

    def place(y, z, c):
        return (c * rows_y + y) * ZRUN + z

    after, before = (me + 1) % count, (me + count - 1) % count
    partner = slot(at_y, at_z, 1 - core)
    y_peers = [slot((at_y + d) % rows_y, at_z, core) for d in range(1, rows_y)]
    z_peers = [slot(at_y, (at_z + d) % ZRUN, core) for d in range(1, ZRUN)]
    x_peers = [half * cols_x + (at_x + d) % cols_x for d in range(1, cols_x)]
    far_peers = [(1 - half) * cols_x + (at_x + d) % cols_x for d in range(cols_x)]
    outer = jnp.where(core == 0, before, after)

    barrier = pltpu.get_barrier_semaphore()
    met = [{"sta": p} for p in x_peers + far_peers]
    met += [{"tm": p} for p in y_peers + z_peers + [partner, outer]]
    for peer in met:
        pl.semaphore_signal(barrier, inc=1, device_id=peer, device_id_type=MESH)

    mine = place(at_y, at_z, core)
    loads = [
        pltpu.make_async_copy(record, rec_buf, load_sem.at[0]),
        pltpu.make_async_copy(templates.at[0], bank.at[mine], load_sem.at[1]),
        pltpu.make_async_copy(shifts, shift_s, load_sem.at[2]),
        pltpu.make_async_copy(live, live_s, load_sem.at[3]),
        pltpu.make_async_copy(plan, plan_s, load_sem.at[4]),
    ]
    for load in loads:
        load.start()

    pl.semaphore_wait(barrier, len(met))

    def piece_copy(src, index, sem, target):
        return pltpu.make_async_remote_copy(
            src_ref=src,
            dst_ref=bank.at[index],
            send_sem=send_sem.at[0],
            recv_sem=recv_sem.at[sem],
            device_id={"tm": target},
            device_id_type=MESH,
        )

    def group_wait(y, first, size, sem):
        group = bank.at[pl.ds(first, size)]
        pltpu.make_async_remote_copy(
            src_ref=group,
            dst_ref=group,
            send_sem=send_sem.at[0],
            recv_sem=recv_sem.at[sem],
            device_id={"tm": me},
            device_id_type=MESH,
        ).wait_recv()

    own = templates.at[0]
    z_steps = list(range(1, ZRUN))
    y_steps = sorted(range(1, rows_y), key=lambda d: -min(d, rows_y - d))
    y_far = [d for d in y_steps if min(d, rows_y - d) > 2]
    y_near = [d for d in y_steps if min(d, rows_y - d) <= 2]

    def z_sem(z):
        return z

    def far_sem(y):
        return ZRUN + y

    def group_sem(y):
        return ZRUN + rows_y + y

    def to_y(d):
        return slot((at_y + d) % rows_y, at_z, core)

    def to_z(d):
        return slot(at_y, (at_z + d) % ZRUN, core)

    for d in y_far:
        piece_copy(own, mine, far_sem(at_y), to_y(d)).start()
    for d in z_steps:
        piece_copy(own, mine, z_sem(at_z), to_z(d)).start()
    for d in y_near:
        piece_copy(own, mine, group_sem(at_y), to_y(d)).start()

    halo_copy = pltpu.make_async_remote_copy(
        src_ref=record,
        dst_ref=halo,
        send_sem=halo_sem.at[0],
        recv_sem=halo_sem.at[1],
        device_id={"tm": before},
        device_id_type=MESH,
    )
    halo_copy.start()

    for back in Z_ORDER:
        z = (at_z + back) % ZRUN
        index = place(at_y, z, core)
        piece_copy(bank.at[index], index, z_sem(z), me).wait_recv()
        for d in y_near:
            piece_copy(bank.at[index], index, group_sem(at_y), to_y(d)).start()
    for back in y_far[::-1]:
        y = (at_y + back) % rows_y
        index = place(y, at_z, core)
        piece_copy(bank.at[index], index, far_sem(y), me).wait_recv()
        for d in z_steps:
            piece_copy(bank.at[index], index, group_sem(y), to_z(d)).start()

    halo_copy.wait_recv()
    for load in loads:
        load.wait()

    row16 = lax.broadcasted_iota(jnp.int32, (16, ext), 0)
    lag = jnp.zeros((16, ext), jnp.int32)
    for c in range(chans):
        lag = jnp.where(row16 == c, shift_s[c], lag)
    tail = jnp.where(me == count - 1, 0.0, halo[...].astype(jnp.float32))
    signal = jnp.concatenate([rec_buf[...].astype(jnp.float32), tail], axis=1)
    signal = jnp.concatenate([signal, jnp.zeros((16 - chans, ext), jnp.float32)], axis=0)
    for bit in range(8):
        signal = jnp.where(
            (lag & (1 << bit)) != 0, shifted_left(signal, 1 << bit), signal
        )
    signal = signal[:, :reach]
    aligned[...] = signal
    energy = signal * signal
    step = 1
    while step < taps:
        energy = energy + shifted_left(energy, step)
        step *= 2
    gain[...] = lax.rsqrt(energy[:, :span] + 1e-06)

    row8 = lax.broadcasted_iota(jnp.int32, (8, reach), 0)
    wide = span + taps // 2

    def build(c, carry):
        lanes = jnp.broadcast_to(aligned[pl.ds(c, 1), :], (8, reach))
        for bit in range(3):
            lanes = jnp.where((row8 & (1 << bit)) != 0, shifted_left(lanes, 1 << bit), lanes)
        lanes = jnp.concatenate([lanes, shifted_left(lanes, 8)], axis=0).astype(jnp.bfloat16)
        for q in range(8):
            pair = shifted_left(lanes, 16 * q)
            hankel[c, 16 * q : 16 * q + 16, :] = pair[:, :wide]
            hankel[c, 128 + 16 * q : 144 + 16 * q, :] = pair[:, 128 : 128 + wide]
        return carry

    lax.fori_loop(0, chans, build, 0, unroll=2)

    def hand_over(y):
        group = bank.at[pl.ds(place(y, 0, core), ZRUN)]
        pltpu.make_async_remote_copy(
            src_ref=group,
            dst_ref=group,
            send_sem=pair_sem.at[0],
            recv_sem=pair_sem.at[1],
            device_id={"tm": partner},
            device_id_type=MESH,
        ).start()

    for d in [0] + y_steps[::-1]:
        y = (at_y + d) % rows_y
        base = place(y, 0, core)
        if d in y_near:
            group_wait(y, base, ZRUN, group_sem(y))
        elif d:
            group_wait(y, base, ZRUN - 1, group_sem(y))
        hand_over(y)

    pieces = rows_y * ZRUN
    theirs = bank.at[pl.ds((1 - core) * pieces, pieces)]
    handed = pltpu.make_async_remote_copy(
        src_ref=theirs,
        dst_ref=theirs,
        send_sem=pair_sem.at[0],
        recv_sem=pair_sem.at[1],
        device_id={"tm": me},
        device_id_type=MESH,
    )
    handed.wait_recv()

    overall = math.sqrt(taps / CHANNELS)
    row12 = lax.broadcasted_iota(jnp.int32, (chans, 1), 0)
    live_col = jnp.zeros((chans, 1), jnp.float32)
    for c in range(chans):
        live_col = jnp.where(row12 == c, live_s[c].astype(jnp.float32) * overall, live_col)

    def widen(p, carry):
        piece = bank[(plan_s[p] % 2) * pieces + plan_s[p] // 2].astype(jnp.float32)
        for part in range(taps // 128):
            wave[part, pl.ds(pl.multiple_of(p * 16, 16), chans), :] = piece[
                :, part * 128 : part * 128 + 128
            ]
        norm = jnp.sum(piece * piece, axis=1, keepdims=True)
        scale = live_col * lax.rsqrt(norm + 1e-06)
        weights[pl.ds(pl.multiple_of(p * 16, 16), chans), :] = jnp.broadcast_to(scale, (chans, 128))
        return carry

    overall = math.sqrt(taps / CHANNELS)
    some = count // ZHALVES

    def stack(first):
        lax.fori_loop(0, some, lambda i, carry: widen(first + i, carry), 0, unroll=16)
        running = jnp.zeros((some, span), jnp.float32)
        for c in range(chans):
            panel = jnp.concatenate(
                [wave[part, pl.ds(first * 16 + c, some, stride=16), :] for part in range(taps // 128)],
                axis=1,
            )
            weight = weights[pl.ds(first * 16 + c, some, stride=16), :]
            weight = jnp.concatenate([weight] * (span // 128), axis=1)
            panel = panel.astype(jnp.bfloat16)
            half_taps = taps // 2
            both = jnp.concatenate([panel[:, :half_taps], panel[:, half_taps:]], axis=0)
            tiles = span // half_taps
            parts = []
            for t in range(tiles + 1):
                rows = both[:some] if t == 0 else both[some:] if t == tiles else both
                parts.append(
                    jnp.dot(
                        rows,
                        hankel[c, :, t * half_taps : (t + 1) * half_taps],
                        preferred_element_type=jnp.float32,
                    )
                )
            corr = jnp.concatenate(
                [parts[t][:some] + parts[t + 1][-some:] for t in range(tiles)], axis=1
            )
            running = running + corr * weight * gain[c : c + 1, :]
        total[pl.ds(pl.multiple_of(first, some), some), :] = running

    per = count // (cols_x * ZHALVES)

    def block(h, x):
        return total.at[pl.ds(pl.multiple_of((h * cols_x + x) * per, per), per), :]

    def row_copy(far, d):
        h = 1 - half if far else half
        kind = 0 if far else 1
        return pltpu.make_async_remote_copy(
            src_ref=block(h, (at_x + d) % cols_x),
            dst_ref=row_recv.at[kind, d],
            send_sem=row_ssem.at[kind, d],
            recv_sem=row_rsem.at[kind, d],
            device_id={"sta": h * cols_x + (at_x + d) % cols_x},
            device_id_type=MESH,
        )

    x_steps = [2, 1, 3, 0] if cols_x == 4 else list(range(cols_x))
    stack((1 - half) * some)
    far_copies = [row_copy(True, d) for d in x_steps]
    for copy in far_copies:
        copy.start()
    stack(half * some)
    near_copies = [row_copy(False, d) for d in x_steps if d]
    for copy in near_copies:
        copy.start()
    sent = bank.at[pl.ds(0, pieces - 1)]
    pltpu.make_async_remote_copy(
        src_ref=sent,
        dst_ref=sent,
        send_sem=send_sem.at[0],
        recv_sem=recv_sem.at[0],
        device_id={"tm": me},
        device_id_type=MESH,
    ).wait_send()
    handed.wait_send()
    halo_copy.wait_send()
    for copy in near_copies:
        copy.wait_recv()
    near = block(half, at_x)[...] + sum(row_recv[1, d] for d in range(1, cols_x))
    for copy in far_copies:
        copy.wait_recv()
    out[...] = near + sum(row_recv[0, d] for d in range(cols_x))
    for copy in far_copies + near_copies:
        copy.wait_send()


def per_device(rows_y, cols_x, record, templates, shifts, live, plan):
    chans, span = record.shape
    taps = templates.shape[2]
    count = plan.shape[0]
    per = count // (cols_x * ZHALVES)
    any_spec = pl.BlockSpec(memory_space=pl.ANY)
    dma = pltpu.SemaphoreType.DMA
    return pl.pallas_call(
        functools.partial(stack_kernel, (rows_y, cols_x, chans, span, taps)),
        out_shape=jax.ShapeDtypeStruct((per, span), jnp.float32),
        in_specs=[any_spec] * 5,
        out_specs=pl.BlockSpec(memory_space=pltpu.VMEM),
        scratch_shapes=[
            pltpu.VMEM((chans, span), jnp.bfloat16),
            pltpu.VMEM((chans, span), jnp.bfloat16),
            pltpu.VMEM((count, chans, taps), jnp.bfloat16),
            pltpu.VMEM((taps // 128, count * 16, 128), jnp.float32),
            pltpu.VMEM((count * 16, 128), jnp.float32),
            pltpu.VMEM((chans, taps // 2, span + taps // 2), jnp.bfloat16),
            pltpu.VMEM((16, span), jnp.float32),
            pltpu.VMEM((16, span + taps), jnp.float32),
            pltpu.VMEM((count, span), jnp.float32),
            pltpu.VMEM((2, cols_x, per, span), jnp.float32),
            pltpu.SMEM(shifts.shape, jnp.int32),
            pltpu.SMEM(live.shape, jnp.int32),
            pltpu.SMEM(plan.shape, jnp.int32),
            dma((5,)),
            dma((2,)),
            dma((1,)),
            dma((ZRUN + 2 * rows_y,)),
            dma((2,)),
            dma((2, cols_x)),
            dma((2, cols_x)),
        ],
        compiler_params=pltpu.CompilerParams(
            collective_id=0, has_side_effects=True, vmem_limit_bytes=67043328
        ),
    )(record, templates, shifts, live, plan)


def solution(mesh):
    cols_x = mesh.shape["sta"] // ZHALVES
    rows_y = mesh.shape["tm"] // (2 * ZRUN)
    placed = (P("sta", "tm"), P("tm", "sta", None), P("sta"), P("sta"), P())
    return jax.shard_map(
        functools.partial(per_device, rows_y, cols_x),
        mesh=mesh,
        in_specs=placed,
        out_specs=P("sta", "tm"),
        check_vma=False,
    )
```

```python
import functools
import math

import jax
import jax.numpy as jnp
from jax import lax
from jax.experimental import pallas as pl
from jax.experimental.pallas import tpu as pltpu
from jax.sharding import PartitionSpec as P

CHANNELS = 96
ZRUN = 4
ZHALVES = 2
Z_ORDER = (1, 3, 2)
MESH = pl.DeviceIdType.MESH


def shifted_left(value, by):
    width = value.shape[1]
    if by % width == 0:
        return value
    return pltpu.roll(value, width - by, 1)


def stack_kernel(
    sizes,
    record,
    templates,
    shifts,
    live,
    plan,
    out,
    rec_buf,
    halo,
    bank,
    wave,
    panels,
    weights,
    hankel,
    gain,
    aligned,
    total,
    row_recv,
    shift_s,
    live_s,
    plan_s,
    load_sem,
    halo_sem,
    send_sem,
    recv_sem,
    pair_sem,
    row_ssem,
    row_rsem,
):
    rows_y, cols_x, chans, span, taps = sizes
    count = rows_y * ZRUN * 2
    ext = 2 * span
    reach = span + taps
    sta = lax.axis_index("sta")
    me = lax.axis_index("tm")
    core = me % 2
    at_z = (me // 2) % ZRUN
    at_y = me // (2 * ZRUN)
    at_x = sta % cols_x
    half = sta // cols_x

    def slot(y, z, c):
        return (y * ZRUN + z) * 2 + c

    def place(y, z, c):
        return (c * rows_y + y) * ZRUN + z

    after, before = (me + 1) % count, (me + count - 1) % count
    partner = slot(at_y, at_z, 1 - core)
    y_peers = [slot((at_y + d) % rows_y, at_z, core) for d in range(1, rows_y)]
    z_peers = [slot(at_y, (at_z + d) % ZRUN, core) for d in range(1, ZRUN)]
    x_peers = [half * cols_x + (at_x + d) % cols_x for d in range(1, cols_x)]
    far_peers = [(1 - half) * cols_x + (at_x + d) % cols_x for d in range(cols_x)]
    outer = jnp.where(core == 0, before, after)

    barrier = pltpu.get_barrier_semaphore()
    met = [{"tm": p} for p in y_peers[2:5] + y_peers[:2] + y_peers[5:] + z_peers + [outer, partner]]
    met += [{"sta": p} for p in far_peers + x_peers]
    for peer in met:
        pl.semaphore_signal(barrier, inc=1, device_id=peer, device_id_type=MESH)

    mine = place(at_y, at_z, core)
    pl.semaphore_wait(barrier, len(met))

    def piece_copy(src, index, sem, target):
        return pltpu.make_async_remote_copy(
            src_ref=src,
            dst_ref=bank.at[index],
            send_sem=send_sem.at[0],
            recv_sem=recv_sem.at[sem],
            device_id={"tm": target},
            device_id_type=MESH,
        )

    def group_wait(y, first, size, sem):
        group = bank.at[pl.ds(first, size)]
        pltpu.make_async_remote_copy(
            src_ref=group,
            dst_ref=group,
            send_sem=send_sem.at[0],
            recv_sem=recv_sem.at[sem],
            device_id={"tm": me},
            device_id_type=MESH,
        ).wait_recv()

    own = templates.at[0]
    z_steps = list(range(1, ZRUN))
    y_steps = sorted(range(1, rows_y), key=lambda d: -min(d, rows_y - d))
    y_far = [d for d in y_steps if min(d, rows_y - d) > 2]
    y_near = [d for d in y_steps if min(d, rows_y - d) <= 2]

    def z_sem(z):
        return z

    def far_sem(y):
        return ZRUN + y

    def group_sem(y):
        return ZRUN + rows_y + y

    def to_y(d):
        return slot((at_y + d) % rows_y, at_z, core)

    def to_z(d):
        return slot(at_y, (at_z + d) % ZRUN, core)

    for d in y_far:
        piece_copy(own, mine, far_sem(at_y), to_y(d)).start()
    for d in z_steps:
        piece_copy(own, mine, z_sem(at_z), to_z(d)).start()
    for d in y_near:
        piece_copy(own, mine, group_sem(at_y), to_y(d)).start()

    loads = [
        pltpu.make_async_copy(record, rec_buf, load_sem.at[0]),
        pltpu.make_async_copy(templates.at[0], bank.at[mine], load_sem.at[1]),
        pltpu.make_async_copy(shifts, shift_s, load_sem.at[2]),
        pltpu.make_async_copy(live, live_s, load_sem.at[3]),
        pltpu.make_async_copy(plan, plan_s, load_sem.at[4]),
    ]
    for load in loads:
        load.start()

    halo_copy = pltpu.make_async_remote_copy(
        src_ref=record,
        dst_ref=halo,
        send_sem=halo_sem.at[0],
        recv_sem=halo_sem.at[1],
        device_id={"tm": before},
        device_id_type=MESH,
    )
    halo_copy.start()

    for back in Z_ORDER:
        z = (at_z + back) % ZRUN
        index = place(at_y, z, core)
        piece_copy(bank.at[index], index, z_sem(z), me).wait_recv()
        for d in y_near:
            piece_copy(bank.at[index], index, group_sem(at_y), to_y(d)).start()
    for back in y_far[::-1]:
        y = (at_y + back) % rows_y
        index = place(y, at_z, core)
        piece_copy(bank.at[index], index, far_sem(y), me).wait_recv()
        for d in z_steps:
            piece_copy(bank.at[index], index, group_sem(y), to_z(d)).start()

    halo_copy.wait_recv()
    for load in loads:
        load.wait()

    row16 = lax.broadcasted_iota(jnp.int32, (16, ext), 0)
    lag = jnp.zeros((16, ext), jnp.int32)
    for c in range(chans):
        lag = jnp.where(row16 == c, shift_s[c], lag)
    tail = jnp.where(me == count - 1, 0.0, halo[...].astype(jnp.float32))
    signal = jnp.concatenate([rec_buf[...].astype(jnp.float32), tail], axis=1)
    signal = jnp.concatenate([signal, jnp.zeros((16 - chans, ext), jnp.float32)], axis=0)
    for bit in range(8):
        signal = jnp.where(
            (lag & (1 << bit)) != 0, shifted_left(signal, 1 << bit), signal
        )
    signal = signal[:, :reach]
    aligned[...] = signal
    energy = signal * signal
    step = 1
    while step < taps:
        energy = energy + shifted_left(energy, step)
        step *= 2
    gain[...] = lax.rsqrt(energy[:, :span] + 1e-06)

    row8 = lax.broadcasted_iota(jnp.int32, (8, reach), 0)
    wide = span + taps // 2

    def build(c, carry):
        lanes = jnp.broadcast_to(aligned[pl.ds(c, 1), :], (8, reach))
        for bit in range(3):
            lanes = jnp.where((row8 & (1 << bit)) != 0, shifted_left(lanes, 1 << bit), lanes)
        lanes = jnp.concatenate([lanes, shifted_left(lanes, 8)], axis=0).astype(jnp.bfloat16)
        for q in range(8):
            pair = shifted_left(lanes, 16 * q)
            hankel[c, 16 * q : 16 * q + 16, :] = pair[:, :wide]
            hankel[c, 128 + 16 * q : 144 + 16 * q, :] = pair[:, 128 : 128 + wide]
        return carry

    lax.fori_loop(0, chans, build, 0, unroll=2)

    def hand_over(y):
        group = bank.at[pl.ds(place(y, 0, core), ZRUN)]
        pltpu.make_async_remote_copy(
            src_ref=group,
            dst_ref=group,
            send_sem=pair_sem.at[0],
            recv_sem=pair_sem.at[1],
            device_id={"tm": partner},
            device_id_type=MESH,
        ).start()

    for d in [0] + y_steps[::-1]:
        y = (at_y + d) % rows_y
        base = place(y, 0, core)
        if d in y_near:
            group_wait(y, base, ZRUN, group_sem(y))
        elif d:
            group_wait(y, base, ZRUN - 1, group_sem(y))
        hand_over(y)

    pieces = rows_y * ZRUN
    theirs = bank.at[pl.ds((1 - core) * pieces, pieces)]
    handed = pltpu.make_async_remote_copy(
        src_ref=theirs,
        dst_ref=theirs,
        send_sem=pair_sem.at[0],
        recv_sem=pair_sem.at[1],
        device_id={"tm": me},
        device_id_type=MESH,
    )
    handed.wait_recv()

    overall = math.sqrt(taps / CHANNELS)
    row12 = lax.broadcasted_iota(jnp.int32, (chans, 1), 0)
    live_col = jnp.zeros((chans, 1), jnp.float32)
    for c in range(chans):
        live_col = jnp.where(row12 == c, live_s[c].astype(jnp.float32) * overall, live_col)

    def widen(p, carry):
        piece = bank[(plan_s[p] % 2) * pieces + plan_s[p] // 2].astype(jnp.float32)
        for part in range(taps // 128):
            wave[part, pl.ds(pl.multiple_of(p * 16, 16), chans), :] = piece[
                :, part * 128 : part * 128 + 128
            ]
        norm = jnp.sum(piece * piece, axis=1, keepdims=True)
        scale = live_col * lax.rsqrt(norm + 1e-06)
        weights[pl.ds(pl.multiple_of(p * 16, 16), chans), :] = jnp.broadcast_to(scale, (chans, 128))
        return carry

    overall = math.sqrt(taps / CHANNELS)
    some = count // ZHALVES

    def stack(first, far, steps):
        lax.fori_loop(0, some, lambda i, carry: widen(first + i, carry), 0, unroll=16)
        width = taps // 2
        tiles = span // width
        held = None
        for t in range(tiles + 1):
            low = jnp.zeros((some, width), jnp.float32)
            high = jnp.zeros((some, width), jnp.float32)
            for c in range(chans):
                if t == 0:
                    panel = jnp.concatenate(
                        [
                            wave[part, pl.ds(first * 16 + c, some, stride=16), :]
                            for part in range(taps // 128)
                        ],
                        axis=1,
                    ).astype(jnp.bfloat16)
                    panels[c, :some] = panel[:, :width]
                    panels[c, some:] = panel[:, width:]
                rows = slice(0, some) if t == 0 else slice(some, None) if t == tiles else slice(None)
                part = jnp.dot(
                    panels[c, rows],
                    hankel[c, :, t * width : (t + 1) * width],
                    preferred_element_type=jnp.float32,
                )
                weight = weights[pl.ds(first * 16 + c, some, stride=16), :]
                weight = jnp.concatenate([weight] * (width // 128), axis=1)
                if t < tiles:
                    low = low + part[:some] * weight * gain[c : c + 1, t * width : (t + 1) * width]
                if t > 0:
                    high = high + part[-some:] * weight * gain[c : c + 1, (t - 1) * width : t * width]
            if t > 0:
                columns = slice((t - 1) * width, t * width)
                total[pl.ds(pl.multiple_of(first, some), some), columns] = held + high
                for d in steps:
                    row_copy(far, d, columns).start()
            held = low

    per = count // (cols_x * ZHALVES)

    def block(h, x, columns):
        return total.at[pl.ds(pl.multiple_of((h * cols_x + x) * per, per), per), columns]

    def row_copy(far, d, columns=slice(None)):
        h = 1 - half if far else half
        kind = 0 if far else 1
        return pltpu.make_async_remote_copy(
            src_ref=block(h, (at_x + d) % cols_x, columns),
            dst_ref=row_recv.at[kind, d, :, columns],
            send_sem=row_ssem.at[kind, d],
            recv_sem=row_rsem.at[kind, d],
            device_id={"sta": h * cols_x + (at_x + d) % cols_x},
            device_id_type=MESH,
        )

    x_steps = [2, 1, 3, 0] if cols_x == 4 else list(range(cols_x))
    stack((1 - half) * some, True, x_steps)
    stack(half * some, False, [d for d in x_steps if d])
    far_copies = [row_copy(True, d) for d in x_steps]
    near_copies = [row_copy(False, d) for d in x_steps if d]
    sent = bank.at[pl.ds(0, pieces - 1)]
    pltpu.make_async_remote_copy(
        src_ref=sent,
        dst_ref=sent,
        send_sem=send_sem.at[0],
        recv_sem=recv_sem.at[0],
        device_id={"tm": me},
        device_id_type=MESH,
    ).wait_send()
    handed.wait_send()
    halo_copy.wait_send()
    for copy in near_copies:
        copy.wait_recv()
    near = block(half, at_x, slice(None))[...] + sum(row_recv[1, d] for d in range(1, cols_x))
    for copy in far_copies:
        copy.wait_recv()
    out[...] = near + sum(row_recv[0, d] for d in range(cols_x))
    for copy in far_copies + near_copies:
        copy.wait_send()


def per_device(rows_y, cols_x, record, templates, shifts, live, plan):
    chans, span = record.shape
    taps = templates.shape[2]
    count = plan.shape[0]
    per = count // (cols_x * ZHALVES)
    any_spec = pl.BlockSpec(memory_space=pl.ANY)
    dma = pltpu.SemaphoreType.DMA
    return pl.pallas_call(
        functools.partial(stack_kernel, (rows_y, cols_x, chans, span, taps)),
        out_shape=jax.ShapeDtypeStruct((per, span), jnp.float32),
        in_specs=[any_spec] * 5,
        out_specs=pl.BlockSpec(memory_space=pltpu.VMEM),
        scratch_shapes=[
            pltpu.VMEM((chans, span), jnp.bfloat16),
            pltpu.VMEM((chans, span), jnp.bfloat16),
            pltpu.VMEM((count, chans, taps), jnp.bfloat16),
            pltpu.VMEM((taps // 128, count * 16, 128), jnp.float32),
            pltpu.VMEM((chans, 2 * (count // ZHALVES), taps // 2), jnp.bfloat16),
            pltpu.VMEM((count * 16, 128), jnp.float32),
            pltpu.VMEM((chans, taps // 2, span + taps // 2), jnp.bfloat16),
            pltpu.VMEM((16, span), jnp.float32),
            pltpu.VMEM((16, span + taps), jnp.float32),
            pltpu.VMEM((count, span), jnp.float32),
            pltpu.VMEM((2, cols_x, per, span), jnp.float32),
            pltpu.SMEM(shifts.shape, jnp.int32),
            pltpu.SMEM(live.shape, jnp.int32),
            pltpu.SMEM(plan.shape, jnp.int32),
            dma((5,)),
            dma((2,)),
            dma((1,)),
            dma((ZRUN + 2 * rows_y,)),
            dma((2,)),
            dma((2, cols_x)),
            dma((2, cols_x)),
        ],
        compiler_params=pltpu.CompilerParams(
            collective_id=0, has_side_effects=True, vmem_limit_bytes=67043328
        ),
    )(record, templates, shifts, live, plan)


def solution(mesh):
    cols_x = mesh.shape["sta"] // ZHALVES
    rows_y = mesh.shape["tm"] // (2 * ZRUN)
    placed = (P("sta", "tm"), P("tm", "sta", None), P("sta"), P("sta"), P())
    return jax.shard_map(
        functools.partial(per_device, rows_y, cols_x),
        mesh=mesh,
        in_specs=placed,
        out_specs=P("sta", "tm"),
        check_vma=False,
    )
```

```python
import functools
import math

import jax
import jax.numpy as jnp
from jax import lax
from jax.experimental import pallas as pl
from jax.experimental.pallas import tpu as pltpu
from jax.sharding import PartitionSpec as P

CHANNELS = 96
ZRUN = 4
ZHALVES = 2
Z_ORDER = (1, 3, 2)
MESH = pl.DeviceIdType.MESH


def shifted_left(value, by):
    width = value.shape[1]
    if by % width == 0:
        return value
    return pltpu.roll(value, width - by, 1)


def stack_kernel(
    sizes,
    record,
    templates,
    shifts,
    live,
    plan,
    out,
    rec_buf,
    halo,
    bank,
    tmpl_buf,
    wave,
    panels,
    weights,
    hankel,
    gain,
    aligned,
    total,
    row_recv,
    shift_s,
    live_s,
    plan_s,
    load_sem,
    halo_sem,
    send_sem,
    recv_sem,
    pair_sem,
    row_ssem,
    row_rsem,
):
    rows_y, cols_x, chans, span, taps = sizes
    count = rows_y * ZRUN * 2
    ext = 2 * span
    reach = span + taps
    sta = lax.axis_index("sta")
    me = lax.axis_index("tm")
    core = me % 2
    at_z = (me // 2) % ZRUN
    at_y = me // (2 * ZRUN)
    at_x = sta % cols_x
    half = sta // cols_x

    def slot(y, z, c):
        return (y * ZRUN + z) * 2 + c

    def place(y, z, c):
        return (c * rows_y + y) * ZRUN + z

    after, before = (me + 1) % count, (me + count - 1) % count
    partner = slot(at_y, at_z, 1 - core)
    y_peers = [slot((at_y + d) % rows_y, at_z, core) for d in range(1, rows_y)]
    z_peers = [slot(at_y, (at_z + d) % ZRUN, core) for d in range(1, ZRUN)]
    x_peers = [half * cols_x + (at_x + d) % cols_x for d in range(1, cols_x)]
    far_peers = [(1 - half) * cols_x + (at_x + d) % cols_x for d in range(cols_x)]
    outer = jnp.where(core == 0, before, after)

    barrier = pltpu.get_barrier_semaphore()
    met = [{"tm": p} for p in y_peers[2:5] + y_peers[:2] + y_peers[5:] + z_peers + [outer, partner]]
    met += [{"sta": p} for p in far_peers + x_peers]
    for peer in met:
        pl.semaphore_signal(barrier, inc=1, device_id=peer, device_id_type=MESH)

    mine = place(at_y, at_z, core)
    fetch = pltpu.make_async_copy(templates.at[0], tmpl_buf, load_sem.at[1])
    fetch.start()
    fetch.wait()
    waves = tmpl_buf[...].astype(jnp.float32)
    cols = taps // 2
    bank[mine] = jnp.concatenate(
        [waves[:8, :cols], waves[:8, cols:], waves[8:, :cols], waves[8:, cols:]], axis=0
    ).astype(jnp.bfloat16)
    pl.semaphore_wait(barrier, len(met))

    def piece_copy(src, index, sem, target):
        return pltpu.make_async_remote_copy(
            src_ref=src,
            dst_ref=bank.at[index],
            send_sem=send_sem.at[0],
            recv_sem=recv_sem.at[sem],
            device_id={"tm": target},
            device_id_type=MESH,
        )

    def group_wait(y, first, size, sem):
        group = bank.at[pl.ds(first, size)]
        pltpu.make_async_remote_copy(
            src_ref=group,
            dst_ref=group,
            send_sem=send_sem.at[0],
            recv_sem=recv_sem.at[sem],
            device_id={"tm": me},
            device_id_type=MESH,
        ).wait_recv()

    own = bank.at[mine]
    z_steps = list(range(1, ZRUN))
    y_steps = sorted(range(1, rows_y), key=lambda d: -min(d, rows_y - d))
    y_far = [d for d in y_steps if min(d, rows_y - d) > 2]
    y_near = [d for d in y_steps if min(d, rows_y - d) <= 2]

    def z_sem(z):
        return z

    def far_sem(y):
        return ZRUN + y

    def group_sem(y):
        return ZRUN + rows_y + y

    def to_y(d):
        return slot((at_y + d) % rows_y, at_z, core)

    def to_z(d):
        return slot(at_y, (at_z + d) % ZRUN, core)

    for d in y_far:
        piece_copy(own, mine, far_sem(at_y), to_y(d)).start()
    for d in z_steps:
        piece_copy(own, mine, z_sem(at_z), to_z(d)).start()
    for d in y_near:
        piece_copy(own, mine, group_sem(at_y), to_y(d)).start()

    loads = [
        pltpu.make_async_copy(record, rec_buf, load_sem.at[0]),
        pltpu.make_async_copy(shifts, shift_s, load_sem.at[2]),
        pltpu.make_async_copy(live, live_s, load_sem.at[3]),
        pltpu.make_async_copy(plan, plan_s, load_sem.at[4]),
    ]
    for load in loads:
        load.start()

    halo_copy = pltpu.make_async_remote_copy(
        src_ref=record,
        dst_ref=halo,
        send_sem=halo_sem.at[0],
        recv_sem=halo_sem.at[1],
        device_id={"tm": before},
        device_id_type=MESH,
    )
    halo_copy.start()

    for back in Z_ORDER:
        z = (at_z + back) % ZRUN
        index = place(at_y, z, core)
        piece_copy(bank.at[index], index, z_sem(z), me).wait_recv()
        for d in y_near:
            piece_copy(bank.at[index], index, group_sem(at_y), to_y(d)).start()
    for back in y_far[::-1]:
        y = (at_y + back) % rows_y
        index = place(y, at_z, core)
        piece_copy(bank.at[index], index, far_sem(y), me).wait_recv()
        for d in z_steps:
            piece_copy(bank.at[index], index, group_sem(y), to_z(d)).start()

    halo_copy.wait_recv()
    for load in loads:
        load.wait()

    row16 = lax.broadcasted_iota(jnp.int32, (16, ext), 0)
    lag = jnp.zeros((16, ext), jnp.int32)
    for c in range(chans):
        lag = jnp.where(row16 == c, shift_s[c], lag)
    tail = jnp.where(me == count - 1, 0.0, halo[...].astype(jnp.float32))
    signal = jnp.concatenate([rec_buf[...].astype(jnp.float32), tail], axis=1)
    signal = jnp.concatenate([signal, jnp.zeros((16 - chans, ext), jnp.float32)], axis=0)
    for bit in range(8):
        signal = jnp.where(
            (lag & (1 << bit)) != 0, shifted_left(signal, 1 << bit), signal
        )
    signal = signal[:, :reach]
    aligned[...] = signal
    energy = signal * signal
    step = 1
    while step < taps:
        energy = energy + shifted_left(energy, step)
        step *= 2
    gain[...] = lax.rsqrt(energy[:, :span] + 1e-06)

    row8 = lax.broadcasted_iota(jnp.int32, (8, reach), 0)
    wide = span + taps // 2

    def build(c, carry):
        lanes = jnp.broadcast_to(aligned[pl.ds(c, 1), :], (8, reach))
        for bit in range(3):
            lanes = jnp.where((row8 & (1 << bit)) != 0, shifted_left(lanes, 1 << bit), lanes)
        lanes = jnp.concatenate([lanes, shifted_left(lanes, 8)], axis=0).astype(jnp.bfloat16)
        for q in range(8):
            pair = shifted_left(lanes, 16 * q)
            hankel[c, 16 * q : 16 * q + 16, :] = pair[:, :wide]
            hankel[c, 128 + 16 * q : 144 + 16 * q, :] = pair[:, 128 : 128 + wide]
        return carry

    lax.fori_loop(0, chans, build, 0, unroll=2)

    def hand_over(y):
        group = bank.at[pl.ds(place(y, 0, core), ZRUN)]
        pltpu.make_async_remote_copy(
            src_ref=group,
            dst_ref=group,
            send_sem=pair_sem.at[0],
            recv_sem=pair_sem.at[1],
            device_id={"tm": partner},
            device_id_type=MESH,
        ).start()

    for d in [0] + y_steps[::-1]:
        y = (at_y + d) % rows_y
        base = place(y, 0, core)
        if d in y_near:
            group_wait(y, base, ZRUN, group_sem(y))
        elif d:
            group_wait(y, base, ZRUN - 1, group_sem(y))
        hand_over(y)

    pieces = rows_y * ZRUN
    theirs = bank.at[pl.ds((1 - core) * pieces, pieces)]
    handed = pltpu.make_async_remote_copy(
        src_ref=theirs,
        dst_ref=theirs,
        send_sem=pair_sem.at[0],
        recv_sem=pair_sem.at[1],
        device_id={"tm": me},
        device_id_type=MESH,
    )
    handed.wait_recv()

    overall = math.sqrt(taps / CHANNELS)
    row12 = lax.broadcasted_iota(jnp.int32, (chans, 1), 0)
    live_col = jnp.zeros((chans, 1), jnp.float32)
    for c in range(chans):
        live_col = jnp.where(row12 == c, live_s[c].astype(jnp.float32) * overall, live_col)

    def widen(p, carry):
        piece = bank[(plan_s[p] % 2) * pieces + plan_s[p] // 2].astype(jnp.float32)
        rest = chans - 8
        for part in range(taps // 128):
            side, col = part // 2, part % 2 * 128
            rows = wave.at[part, pl.ds(pl.multiple_of(p * 16, 16), 16), :]
            rows[:8, :] = piece[8 * side : 8 * side + 8, col : col + 128]
            rows[8 + rest * side : 8 + rest * (side + 1), :] = piece[
                16 + rest * side : 16 + rest * (side + 1), col : col + 128
            ]
        norm = jnp.sum(piece * piece, axis=1, keepdims=True)
        norm = jnp.concatenate([norm[:8] + norm[8:16], norm[16:20] + norm[20:24]], axis=0)
        scale = live_col * lax.rsqrt(norm + 1e-06)
        weights[pl.ds(pl.multiple_of(p * 16, 16), chans), :] = jnp.broadcast_to(scale, (chans, 128))
        return carry

    overall = math.sqrt(taps / CHANNELS)
    some = count // ZHALVES

    def stack(first, far, steps):
        lax.fori_loop(0, some, lambda i, carry: widen(first + i, carry), 0, unroll=16)
        width = taps // 2
        tiles = span // width
        held = None
        for t in range(tiles + 1):
            low = jnp.zeros((some, width), jnp.float32)
            high = jnp.zeros((some, width), jnp.float32)
            for c in range(chans):
                if t == 0:
                    panel = jnp.concatenate(
                        [
                            wave[
                                part,
                                pl.ds(
                                    first * 16 + c + (4 if part >= 2 and c >= 8 else 0), some, stride=16
                                ),
                                :,
                            ]
                            for part in range(taps // 128)
                        ],
                        axis=1,
                    ).astype(jnp.bfloat16)
                    panels[c, :some] = panel[:, :width]
                    panels[c, some:] = panel[:, width:]
                rows = slice(0, some) if t == 0 else slice(some, None) if t == tiles else slice(None)
                part = jnp.dot(
                    panels[c, rows],
                    hankel[c, :, t * width : (t + 1) * width],
                    preferred_element_type=jnp.float32,
                )
                weight = weights[pl.ds(first * 16 + c, some, stride=16), :]
                weight = jnp.concatenate([weight] * (width // 128), axis=1)
                if t < tiles:
                    low = low + part[:some] * weight * gain[c : c + 1, t * width : (t + 1) * width]
                if t > 0:
                    high = high + part[-some:] * weight * gain[c : c + 1, (t - 1) * width : t * width]
            if t > 0:
                columns = slice((t - 1) * width, t * width)
                total[pl.ds(pl.multiple_of(first, some), some), columns] = held + high
                for d in steps:
                    row_copy(far, d, columns).start()
            held = low

    per = count // (cols_x * ZHALVES)

    def block(h, x, columns):
        return total.at[pl.ds(pl.multiple_of((h * cols_x + x) * per, per), per), columns]

    def row_copy(far, d, columns=slice(None)):
        h = 1 - half if far else half
        kind = 0 if far else 1
        return pltpu.make_async_remote_copy(
            src_ref=block(h, (at_x + d) % cols_x, columns),
            dst_ref=row_recv.at[kind, d, :, columns],
            send_sem=row_ssem.at[kind, d],
            recv_sem=row_rsem.at[kind, d],
            device_id={"sta": h * cols_x + (at_x + d) % cols_x},
            device_id_type=MESH,
        )

    x_steps = [2, 1, 3, 0] if cols_x == 4 else list(range(cols_x))
    stack((1 - half) * some, True, x_steps)
    stack(half * some, False, [d for d in x_steps if d])
    far_copies = [row_copy(True, d) for d in x_steps]
    near_copies = [row_copy(False, d) for d in x_steps if d]
    sent = bank.at[pl.ds(0, pieces - 1)]
    pltpu.make_async_remote_copy(
        src_ref=sent,
        dst_ref=sent,
        send_sem=send_sem.at[0],
        recv_sem=recv_sem.at[0],
        device_id={"tm": me},
        device_id_type=MESH,
    ).wait_send()
    handed.wait_send()
    halo_copy.wait_send()
    for copy in near_copies:
        copy.wait_recv()
    near = block(half, at_x, slice(None))[...] + sum(row_recv[1, d] for d in range(1, cols_x))
    for copy in far_copies:
        copy.wait_recv()
    out[...] = near + sum(row_recv[0, d] for d in range(cols_x))
    for copy in far_copies + near_copies:
        copy.wait_send()


def per_device(rows_y, cols_x, record, templates, shifts, live, plan):
    chans, span = record.shape
    taps = templates.shape[2]
    count = plan.shape[0]
    per = count // (cols_x * ZHALVES)
    any_spec = pl.BlockSpec(memory_space=pl.ANY)
    dma = pltpu.SemaphoreType.DMA
    return pl.pallas_call(
        functools.partial(stack_kernel, (rows_y, cols_x, chans, span, taps)),
        out_shape=jax.ShapeDtypeStruct((per, span), jnp.float32),
        in_specs=[any_spec] * 5,
        out_specs=pl.BlockSpec(memory_space=pltpu.VMEM),
        scratch_shapes=[
            pltpu.VMEM((chans, span), jnp.bfloat16),
            pltpu.VMEM((chans, span), jnp.bfloat16),
            pltpu.VMEM((count, 2 * chans, taps // 2), jnp.bfloat16),
            pltpu.VMEM((chans, taps), jnp.bfloat16),
            pltpu.VMEM((taps // 128, count * 16, 128), jnp.float32),
            pltpu.VMEM((chans, 2 * (count // ZHALVES), taps // 2), jnp.bfloat16),
            pltpu.VMEM((count * 16, 128), jnp.float32),
            pltpu.VMEM((chans, taps // 2, span + taps // 2), jnp.bfloat16),
            pltpu.VMEM((16, span), jnp.float32),
            pltpu.VMEM((16, span + taps), jnp.float32),
            pltpu.VMEM((count, span), jnp.float32),
            pltpu.VMEM((2, cols_x, per, span), jnp.float32),
            pltpu.SMEM(shifts.shape, jnp.int32),
            pltpu.SMEM(live.shape, jnp.int32),
            pltpu.SMEM(plan.shape, jnp.int32),
            dma((5,)),
            dma((2,)),
            dma((1,)),
            dma((ZRUN + 2 * rows_y,)),
            dma((2,)),
            dma((2, cols_x)),
            dma((2, cols_x)),
        ],
        compiler_params=pltpu.CompilerParams(
            collective_id=0, has_side_effects=True, vmem_limit_bytes=67043328
        ),
    )(record, templates, shifts, live, plan)


def solution(mesh):
    cols_x = mesh.shape["sta"] // ZHALVES
    rows_y = mesh.shape["tm"] // (2 * ZRUN)
    placed = (P("sta", "tm"), P("tm", "sta", None), P("sta"), P("sta"), P())
    return jax.shard_map(
        functools.partial(per_device, rows_y, cols_x),
        mesh=mesh,
        in_specs=placed,
        out_specs=P("sta", "tm"),
        check_vma=False,
    )
```
